32 devices in a mesh: row: 2 (over y), col: 4 (over z), layer: 4 (over x, core).
Axes of the slice: x: 2, y: 2, z: 4, core: 2. Of those that a mesh axis runs over, the one named last changes fastest.
Arguments:
- integrals: bfloat16 [64, 1024, 768], P('layer', 'col', 'row'), may hold values from -0.0234375 to 0.0234375
- amplitudes: bfloat16 [64, 1024, 512], P('layer', 'row', 'col'), may hold values from -6 to 6
- coulomb: bfloat16 [768, 512], P(('row', 'layer'), 'col'), may hold values from -6 to 6
- row_gap: float32 [768], P(('row', 'layer')), may hold values from 0.5 to 4
- col_gap: float32 [512], P('col'), may hold values from 0.5 to 4
Outputs:
- residual: float32 [768, 512], P(('row', 'layer'), 'col')
The draws below stay inside these ranges and needn't reach their ends.
All inputs are finite; a program needn't handle non-finite values.
Results may differ from the reference program's by a relative error of at most 0.0003.
Values may be sent and summed in bfloat16 or wider, within the bound.
A program may use at most 64 MiB of HBM per device.

```python
import math
import jax
import jax.numpy as jnp

OCC = 64
VIR = 1024
NROW = 768
NCOL = 512


def levels(own_key, shape, split, low, top_value):
    def one(dim, blocks):
        heights = jax.random.uniform(jax.random.fold_in(jax.random.fold_in(own_key, 6), dim), (blocks,), jnp.float32, low / len(split), top_value / len(split))
        return jnp.repeat(jnp.exp(heights), shape[dim] // blocks).reshape((-1,) + (1,) * (len(shape) - dim - 1))

    gain = one(*split[0])
    for cut in split[1:]:
        gain = gain * one(*cut)
    return gain


def scatter_about(key, dims, deviation, bound, cuts=(), dtype=jnp.bfloat16):
    factor_of = levels(key, dims, cuts, -0.22, 0.18) if cuts else 1.0
    entries = jax.random.normal(key, dims, jnp.float32) * deviation * factor_of
    return jnp.minimum(jnp.maximum(entries, -bound), bound).astype(dtype)


def setup_inputs(seed: int = 0) -> dict:
    key_of = jax.random.split(jax.random.key(seed), 6)
    return {
        "integrals": scatter_about(key_of[0], (OCC, VIR, NROW), (OCC * VIR) ** -0.5, 0.0234375, ((0, 4), (1, 4), (2, 2))),
        "amplitudes": scatter_about(key_of[1], (OCC, VIR, NCOL), 1.0, 6.0, ((0, 4), (1, 2), (2, 4))),
        "coulomb": scatter_about(key_of[2], (NROW, NCOL), 1.0, 6.0, ((0, 8), (1, 4))),
        "row_gap": jnp.clip(jnp.exp(math.log(4.0) - 2.0794415 * jax.random.uniform(key_of[3], (NROW,), jnp.float32) ** levels(key_of[3], (NROW,), ((0, 8),), -0.2, 0.2)), 0.5, 4.0),
        "col_gap": jnp.clip(jnp.exp(math.log(4.0) - 2.0794415 * jax.random.uniform(key_of[4], (NCOL,), jnp.float32) ** levels(key_of[4], (NCOL,), ((0, 4),), -0.2, 0.2)), 0.5, 4.0),
    }


def reference(integrals, amplitudes, coulomb, row_gap, col_gap):
    left_matrix = integrals.reshape(OCC * VIR, NROW)
    right_matrix = amplitudes.reshape(OCC * VIR, NCOL)
    product = jnp.dot(left_matrix.T, right_matrix, preferred_element_type=jnp.float32)
    gap_sum = row_gap[:, None] + col_gap[None, :]
    return (coulomb.astype(jnp.float32) + product) / gap_sum
```

```python
import functools

import jax
import jax.numpy as jnp
from jax import lax
from jax.experimental import pallas as pl
from jax.experimental.pallas import tpu as pltpu
from jax.sharding import PartitionSpec as P

CHUNKS = 8


def kernel(R, C, L, Q, i_ref, a_ref, coul_ref, rgap_ref, cgap_ref, o_ref,
           a_all, az, relay, i_buf, i_t, acc, lay_buf, col_buf,
           ysend, yrecv, zsend, zrecv, hsend, hrecv, fsend, frecv, isem,
           lsend, lrecv, csend, crecv):
    r, c, l = lax.axis_index("row"), lax.axis_index("col"), lax.axis_index("layer")
    K, V_row, N = a_ref.shape
    V = i_ref.shape[1]
    M = i_ref.shape[2]
    kc = K // Q
    m = C // R
    half = V // 2
    rows = M // L
    stages = L.bit_length() - 1
    far = C // 2 if C % 2 == 0 and C >= 4 else 0

    def dev(row=None, col=None, layer=None):
        return {"row": r if row is None else row, "col": c if col is None else col, "layer": l if layer is None else layer}

    def remote(src, dst, ss, rs, to):
        return pltpu.make_async_remote_copy(src_ref=src, dst_ref=dst, send_sem=ss, recv_sem=rs,
                                            device_id=to, device_id_type=pl.DeviceIdType.MESH)

    def ks(q):
        return pl.ds(q * kc, kc)

    def near(dc):
        return lax.rem(c + dc + C, C)

    def i_copy(q):
        return pltpu.make_async_copy(i_ref.at[ks(q)], i_buf.at[ks(q)], isem.at[q])

    def own_copy(q):
        return pltpu.make_async_copy(a_ref.at[ks(q)], a_all.at[r, ks(q)], yrecv.at[r, q])

    for q in range(Q):
        own_copy(q).start()
        i_copy(q).start()

    barrier = pltpu.get_barrier_semaphore()
    partners = [dev(row=lax.rem(r + d, R)) for d in range(1, R)]
    partners += [dev(col=near(d)) for d in range(1, C)]
    partners += [dev(layer=l ^ (1 << t)) for t in range(stages)]
    for p in partners:
        pl.semaphore_signal(barrier, inc=1, device_id=p, device_id_type=pl.DeviceIdType.MESH)
    pl.semaphore_wait(barrier, len(partners))

    def y_copy(d, q):
        to = lax.rem(r + d, R)
        return remote(a_ref.at[ks(q)], a_all.at[r, ks(q)], ysend.at[d, q], yrecv.at[r, q], dev(row=to))

    def y_wait(d, q):
        s = lax.rem(r + d, R)
        remote(a_ref.at[ks(q)], a_all.at[s, ks(q)], ysend.at[0, q], yrecv.at[s, q], dev(row=s)).wait_recv()

    def z_copies(dc, q, src, offset):
        b = near(dc)
        if far and dc == far:
            out = []
            for side in range(2):
                part = src.at[ks(q), pl.ds(pl.multiple_of(offset + side * half, half), half)]
                out.append(remote(part, relay.at[side, ks(q)], hsend.at[side, q], hrecv.at[side, q],
                                  dev(col=near(1 - 2 * side))))
            return out
        part = src.at[ks(q), pl.ds(pl.multiple_of(offset, V), V)]
        return [remote(part, az.at[c, ks(q)], zsend.at[dc, q], zrecv.at[c, q], dev(col=b))]

    order = ([far] if far else []) + [d for k in range(1, C) for d in ((k, C - k) if k < C - k else (k,) if k == C - k else ()) if d != far]

    for q in range(Q):
        for d in range(1, R):
            y_copy(d, q).start()
        for dc in order:
            b = near(dc)

            @pl.when(lax.div(b, m) == r)
            def _():
                for cp in z_copies(dc, q, a_ref, lax.rem(b, m) * V):
                    cp.start()

    def late(q):
        for d in range(1, R):
            y_wait(d, q)
        for dc in order:
            b = near(dc)

            @pl.when(lax.div(b, m) != r)
            def _():
                for cp in z_copies(dc, q, a_all.at[lax.div(b, m)], lax.rem(b, m) * V):
                    cp.start()

    def forward_copy(side, q):
        s = near(-1 + 2 * side)
        to = near((far - 1) * (1 - 2 * side))
        return remote(relay.at[side, ks(q)], az.at[s, ks(q), pl.ds(side * half, half)],
                      fsend.at[side, q], frecv.at[side, q], dev(col=to))

    def forward(q):
        if not far:
            return
        for side in range(2):
            remote(relay.at[side, ks(q)], relay.at[side, ks(q)], hsend.at[side, q], hrecv.at[side, q],
                   dev(col=near(1))).wait_recv()
            forward_copy(side, q).start()

    def add(block, x, q):
        w = kc * V
        part = lax.dot_general(i_t[:, q * w:(q + 1) * w], x.reshape(w, N), (((1,), (0,)), ((), ())),
                               preferred_element_type=jnp.float32)
        for lb in range(L):
            piece = part[lb * rows:(lb + 1) * rows]
            if q == 0:
                acc[lb, block] = piece
            else:
                acc[lb, block] += piece

    def own_product(q):
        i_copy(q).wait()
        for k in range(kc):
            at = (q * kc + k) * V
            i_t[:, at:at + V] = i_buf[q * kc + k].T
        own_copy(q).wait()
        x = a_all[lax.div(c, m), ks(q), pl.ds(pl.multiple_of(lax.rem(c, m) * V, V), V)]
        add(c, x, q)

    def arrived(q):
        for dc in order[::-1]:
            s = near(-dc)
            if far and dc == far:
                for side in range(2):
                    dst = az.at[s, ks(q), pl.ds(side * half, half)]
                    remote(dst, dst, fsend.at[side, q], frecv.at[side, q], dev(col=near(1))).wait_recv()
            else:
                remote(az.at[s, ks(q)], az.at[s, ks(q)], zsend.at[dc, q], zrecv.at[s, q], dev(col=near(1))).wait_recv()
            add(s, az[s, ks(q)], q)

    for step in range(Q + 2):
        if step < Q:
            late(step)
        if 1 <= step <= Q:
            forward(step - 1)
        if step < Q:
            own_product(step)
        if step >= 2:
            arrived(step - 2)

    c_order = order + [0]

    def block(t, hi, bit):
        return (hi << (t + 1)) | (bit << t) | (l & ((1 << t) - 1))

    def hi_order(n):
        if n == 1:
            return [0]
        below = hi_order(n // 2)
        return [2 * x + 1 for x in below] + [2 * x for x in below]

    def halving(t, i, dc):
        n = L >> (t + 1)
        hi = (l >> (t + 1)) ^ hi_order(n)[i]
        bit = (l >> t) & 1
        col = near(dc)
        slot = n - 1 + hi
        sem = (slot, col)
        return (remote(acc.at[block(t, hi, 1 - bit), col], lay_buf.at[slot, col], lsend.at[sem], lrecv.at[sem],
                       dev(layer=l ^ (1 << t))), block(t, hi, bit), slot, col)

    def final_copy(dc):
        return remote(acc.at[l, near(dc)], col_buf.at[c], csend.at[dc], crecv.at[c], dev(col=near(dc)))

    for i in range(L >> 1):
        for dc in c_order:
            halving(0, i, dc)[0].start()
    for t in range(stages):
        for i in range(L >> (t + 1)):
            for dc in c_order:
                cp, keep, slot, col = halving(t, i, dc)
                cp.wait_recv()
                acc[keep, col] += lay_buf[slot, col]
                if t + 1 < stages:
                    n = L >> (t + 2)
                    if i < n:
                        halving(t + 1, i, dc)[0].start()
                elif dc:
                    final_copy(dc).start()

    total = acc[l, c]
    for dc in order[::-1]:
        s = near(-dc)
        remote(col_buf.at[s], col_buf.at[s], csend.at[dc], crecv.at[s], dev(col=near(1))).wait_recv()
        total += col_buf[s]
    o_ref[...] = (coul_ref[...].astype(jnp.float32) + total) / (rgap_ref[...] + cgap_ref[...])

    for q in range(Q):
        for d in range(1, R):
            y_copy(d, q).wait_send()
        for dc in order:
            for cp in z_copies(dc, q, a_ref, 0):
                cp.wait_send()
        if far:
            for side in range(2):
                forward_copy(side, q).wait_send()
    for t in range(stages):
        for i in range(L >> (t + 1)):
            for dc in c_order:
                halving(t, i, dc)[0].wait_send()
    for dc in order:
        final_copy(dc).wait_send()


def local(R, C, L, integrals, amplitudes, coulomb, row_gap, col_gap):
    K, V, M = integrals.shape
    V_row, N = amplitudes.shape[1:]
    rows = M // L
    Q = CHUNKS
    while K % Q:
        Q -= 1
    slots = L - 1
    dma = pltpu.SemaphoreType.DMA
    vmem = pl.BlockSpec(memory_space=pltpu.VMEM)
    anyspace = pl.BlockSpec(memory_space=pl.ANY)
    return pl.pallas_call(
        functools.partial(kernel, R, C, L, Q),
        out_shape=jax.ShapeDtypeStruct((rows, N), jnp.float32),
        in_specs=[anyspace, anyspace, vmem, vmem, vmem],
        out_specs=vmem,
        scratch_shapes=[
            pltpu.VMEM((R, K, V_row, N), jnp.bfloat16),
            pltpu.VMEM((C, K, V, N), jnp.bfloat16),
            pltpu.VMEM((2, K, V // 2, N), jnp.bfloat16),
            pltpu.VMEM((K, V, M), jnp.bfloat16),
            pltpu.VMEM((M, K * V), jnp.bfloat16),
            pltpu.VMEM((L, C, rows, N), jnp.float32),
            pltpu.VMEM((slots, C, rows, N), jnp.float32),
            pltpu.VMEM((C, rows, N), jnp.float32),
            dma((R, Q)), dma((R, Q)),
            dma((C, Q)), dma((C, Q)),
            dma((2, Q)), dma((2, Q)),
            dma((2, Q)), dma((2, Q)),
            dma((Q,)),
            dma((slots, C)), dma((slots, C)),
            dma((C,)), dma((C,)),
        ],
        compiler_params=pltpu.CompilerParams(collective_id=0, has_side_effects=True),
    )(integrals, amplitudes, coulomb, row_gap[:, None], col_gap[None, :])


def solution(mesh):
    R, C, L = (mesh.shape[a] for a in ("row", "col", "layer"))
    placed = (
        P("layer", "col", "row"),
        P("layer", "row", "col"),
        P(("row", "layer"), "col"),
        P(("row", "layer")),
        P("col"),
    )
    return jax.shard_map(
        functools.partial(local, R, C, L), mesh=mesh, in_specs=placed, out_specs=P(("row", "layer"), "col"),
        check_vma=False,
    )
```

```python
import functools

import jax
import jax.numpy as jnp
from jax import lax
from jax.experimental import pallas as pl
from jax.experimental.pallas import tpu as pltpu
from jax.sharding import PartitionSpec as P

MESH = pl.DeviceIdType.MESH


def hi_order(n):
    if n == 1:
        return [0]
    below = hi_order(n // 2)
    return [2 * x + 1 for x in below] + [2 * x for x in below]


def kernel(R, C, L, Q, i_ref, a_ref, coul_ref, rgap_ref, cgap_ref, o_ref,
           a_all, az, i_all, i_t, acc, lay_buf, row_buf, col_buf,
           asend, arecv, xsend, xrecv, zsend, zrecv,
           osend, orecv, lsend, lrecv, rsend, rrecv, csend, crecv):
    r, c, l = lax.axis_index("row"), lax.axis_index("col"), lax.axis_index("layer")
    K, V_row, N = a_ref.shape
    V, M = i_ref.shape[1:]
    Kr = K // R
    kc = Kr // Q
    m = C // R
    w = kc * V
    rows = M // L
    stages = L.bit_length() - 1

    def remote(src, dst, ss, rs, **to):
        where = {"row": r, "col": c, "layer": l}
        where.update(to)
        return pltpu.make_async_remote_copy(src_ref=src, dst_ref=dst, send_sem=ss, recv_sem=rs,
                                            device_id=where, device_id_type=MESH)

    def ks(q):
        return pl.ds(q * kc, kc)

    def far_row(d):
        return lax.rem(r + d, R)

    def near(dc):
        return lax.rem(c + dc + C, C)

    order = sorted(range(1, C), key=lambda d: -min(d, C - d))

    def slice_for(d, q):
        return pl.ds(far_row(d) * Kr + q * kc, kc)

    def own_a(q):
        return pltpu.make_async_copy(a_ref.at[slice_for(0, q)], a_all.at[0, ks(q)], arecv.at[0, q])

    def own_i(q):
        return pltpu.make_async_copy(i_ref.at[slice_for(0, q)], i_all.at[0, ks(q)], xrecv.at[0, q])

    for q in range(Q):
        own_a(q).start()
        own_i(q).start()

    barrier = pltpu.get_barrier_semaphore()
    partners = [{"row": far_row(d)} for d in range(1, R)]
    partners += [{"col": near(d)} for d in range(1, C)]
    partners += [{"layer": l ^ (1 << t)} for t in range(stages)]
    for p in partners:
        where = {"row": r, "col": c, "layer": l}
        where.update(p)
        pl.semaphore_signal(barrier, inc=1, device_id=where, device_id_type=MESH)
    pl.semaphore_wait(barrier, len(partners))

    def row_a(d, q):
        return remote(a_ref.at[slice_for(d, q)], a_all.at[R - d, ks(q)], asend.at[d, q], arecv.at[R - d, q], row=far_row(d))

    def row_i(d, q):
        return remote(i_ref.at[slice_for(d, q)], i_all.at[R - d, ks(q)], xsend.at[d, q], xrecv.at[R - d, q], row=far_row(d))

    def col_a(d, j, q):
        b = far_row(d) * m + j
        at = pl.ds(j * V, V)
        src = a_all.at[d, ks(q), at] if d else a_ref.at[slice_for(0, q), at]
        return b, remote(src, az.at[c, ks(q)], zsend.at[d, j, q], zrecv.at[c, q], col=b)

    def col_start(d, q):
        for j in range(m):
            b, cp = col_a(d, j, q)

            @pl.when(b != c)
            def _():
                cp.start()

    for q in range(Q):
        for d in range(1, R):
            row_a(d, q).start()
        col_start(0, q)
    for q in range(Q):
        for d in range(1, R):
            row_i(d, q).start()

    def turn(d, q):
        for k in range(kc):
            at = (q * kc + k) * V
            i_t[d, :, at:at + V] = i_all[d, q * kc + k].T

    def add(d, block, x, q):
        part = lax.dot_general(i_t[d, :, q * w:(q + 1) * w], x, (((1,), (0,)), ((), ())),
                               preferred_element_type=jnp.float32)
        for lb in range(L):
            piece = part[lb * rows:(lb + 1) * rows]
            if q == 0:
                acc[d, lb, block] = piece
            else:
                acc[d, lb, block] += piece

    own_row = lax.rem(lax.div(c, m) - r + R, R)
    own_at = pl.ds(pl.multiple_of(lax.rem(c, m) * V, V), V)

    def own_block(d, q):
        add(d, c, a_all[own_row, ks(q), own_at].reshape(w, N), q)

    for q in range(Q):
        own_a(q).wait()
        for d in range(1, R):
            row_a(R - d, q).wait_recv()
            col_start(d, q)
        own_i(q).wait()
        turn(0, q)
        own_block(0, q)

    for q in range(Q):
        for dc in order[::-1]:
            s = near(dc)
            here = az.at[s, ks(q)]
            remote(here, here, zsend.at[0, 0, q], zrecv.at[s, q], col=s).wait_recv()
            add(0, s, az[s, ks(q)].reshape(w, N), q)

    def block(t, hi, bit):
        return (hi << (t + 1)) | (bit << t) | (l & ((1 << t) - 1))

    def halving(d, t, i, col):
        n = L >> (t + 1)
        hi = (l >> (t + 1)) ^ hi_order(n)[i]
        bit = (l >> t) & 1
        slot = n - 1 + hi
        give, keep = block(t, hi, 1 - bit), block(t, hi, bit)
        if d == 0:
            cp = remote(acc.at[0, give], lay_buf.at[0, slot], osend.at[slot], orecv.at[slot], layer=l ^ (1 << t))
        else:
            cp = remote(acc.at[d, give, col], lay_buf.at[d, slot, col], lsend.at[d, slot, col], lrecv.at[d, slot, col],
                        layer=l ^ (1 << t))
        return cp, keep, slot

    def own_stage(t):
        for i in range(L >> (t + 1)):
            cp, keep, slot = halving(0, t, i, None)
            cp.wait_recv()
            acc[0, keep] += lay_buf[0, slot]
            if t + 1 < stages and i < L >> (t + 2):
                halving(0, t + 1, i, None)[0].start()

    for i in range(L >> 1):
        halving(0, 0, i, None)[0].start()

    for q in range(Q):
        for d in range(1, R):
            row_i(R - d, q).wait_recv()
            turn(d, q)
            own_block(d, q)
            for dc in order:
                s = near(dc)
                add(d, s, az[s, ks(q)].reshape(w, N), q)
        if q == 0:
            own_stage(0)

    c_order = [near(dc) for dc in order] + [c]

    def row_sum(d, col):
        return remote(acc.at[d, l, col], row_buf.at[R - d, col], rsend.at[d, col], rrecv.at[R - d, col], row=far_row(d))

    def col_sum(dc):
        return remote(acc.at[0, l, near(dc)], col_buf.at[c], csend.at[dc], crecv.at[c], col=near(dc))

    for i in range(L >> 1):
        for d in range(1, R):
            for col in c_order:
                halving(d, 0, i, col)[0].start()
    for t in range(1, stages):
        own_stage(t)
    for t in range(stages):
        for i in range(L >> (t + 1)):
            for d in range(1, R):
                for col in c_order:
                    cp, keep, slot = halving(d, t, i, col)
                    cp.wait_recv()
                    acc[d, keep, col] += lay_buf[d, slot, col]
                    if t + 1 == stages:
                        row_sum(d, col).start()
                    elif i < L >> (t + 2):
                        halving(d, t + 1, i, col)[0].start()
    for at, col in enumerate(c_order):
        for d in range(1, R):
            row_sum(R - d, col).wait_recv()
            acc[0, l, col] += row_buf[d, col]
        if at < C - 1:
            col_sum(order[at]).start()

    total = acc[0, l, c]
    for dc in order[::-1]:
        s = near(dc)
        remote(col_buf.at[s], col_buf.at[s], csend.at[dc], crecv.at[s], col=s).wait_recv()
        total += col_buf[s]
    o_ref[...] = (coul_ref[...].astype(jnp.float32) + total) / (rgap_ref[...] + cgap_ref[...])

    for q in range(Q):
        for d in range(R):
            if d:
                row_a(d, q).wait_send()
                row_i(d, q).wait_send()
            for j in range(m):
                b, cp = col_a(d, j, q)

                @pl.when(b != c)
                def _():
                    cp.wait_send()
    for t in range(stages):
        for i in range(L >> (t + 1)):
            halving(0, t, i, None)[0].wait_send()
            for d in range(1, R):
                for col in c_order:
                    halving(d, t, i, col)[0].wait_send()
    for col in c_order:
        for d in range(1, R):
            row_sum(d, col).wait_send()
    for dc in order:
        col_sum(dc).wait_send()


def local(R, C, L, integrals, amplitudes, coulomb, row_gap, col_gap):
    K, V, M = integrals.shape
    V_row, N = amplitudes.shape[1:]
    rows = M // L
    Kr = K // R
    Q = Kr
    m = C // R
    slots = L - 1
    dma = pltpu.SemaphoreType.DMA
    vmem = pl.BlockSpec(memory_space=pltpu.VMEM)
    anyspace = pl.BlockSpec(memory_space=pl.ANY)
    return pl.pallas_call(
        functools.partial(kernel, R, C, L, Q),
        out_shape=jax.ShapeDtypeStruct((rows, N), jnp.float32),
        in_specs=[anyspace, anyspace, vmem, vmem, vmem],
        out_specs=vmem,
        scratch_shapes=[
            pltpu.VMEM((R, Kr, V_row, N), jnp.bfloat16),
            pltpu.VMEM((C, Kr, V, N), jnp.bfloat16),
            pltpu.VMEM((R, Kr, V, M), jnp.bfloat16),
            pltpu.VMEM((R, M, Kr * V), jnp.bfloat16),
            pltpu.VMEM((R, L, C, rows, N), jnp.float32),
            pltpu.VMEM((R, slots, C, rows, N), jnp.float32),
            pltpu.VMEM((R, C, rows, N), jnp.float32),
            pltpu.VMEM((C, rows, N), jnp.float32),
            dma((R, Q)), dma((R, Q)),
            dma((R, Q)), dma((R, Q)),
            dma((R, m, Q)), dma((C, Q)),
            dma((slots,)), dma((slots,)),
            dma((R, slots, C)), dma((R, slots, C)),
            dma((R, C)), dma((R, C)),
            dma((C,)), dma((C,)),
        ],
        compiler_params=pltpu.CompilerParams(collective_id=0, has_side_effects=True),
    )(integrals, amplitudes, coulomb, row_gap[:, None], col_gap[None, :])


def solution(mesh):
    R, C, L = (mesh.shape[a] for a in ("row", "col", "layer"))
    placed = (
        P("layer", "col", "row"),
        P("layer", "row", "col"),
        P(("row", "layer"), "col"),
        P(("row", "layer")),
        P("col"),
    )
    return jax.shard_map(
        functools.partial(local, R, C, L), mesh=mesh, in_specs=placed, out_specs=P(("row", "layer"), "col"),
        check_vma=False,
    )
```

```python
import functools

import jax
import jax.numpy as jnp
from jax import lax
from jax.experimental import pallas as pl
from jax.experimental.pallas import tpu as pltpu
from jax.sharding import PartitionSpec as P

MESH = pl.DeviceIdType.MESH


def hi_order(n):
    if n == 1:
        return [0]
    below = hi_order(n // 2)
    return [2 * x + 1 for x in below] + [2 * x for x in below]


def kernel(R, C, L, Q, i_ref, a_ref, o_ref,
           a_all, az, i_all, i_t, acc, lay_buf, row_buf, col_buf,
           asend, arecv, xsend, xrecv, zsend, zrecv,
           osend, orecv, lsend, lrecv, rsend, rrecv, csend, crecv):
    r, c, l = lax.axis_index("row"), lax.axis_index("col"), lax.axis_index("layer")
    K, V_row, N = a_ref.shape
    V, M = i_ref.shape[1:]
    Kr = K // R
    kc = Kr // Q
    m = C // R
    w = kc * V
    rows = M // L
    stages = L.bit_length() - 1
    late = M // 2 // 128 * 128 if stages == 2 and M % 128 == 0 else 0
    early = M - late
    top = l >> (stages - 1)

    def remote(src, dst, ss, rs, **to):
        where = {"row": r, "col": c, "layer": l}
        where.update(to)
        return pltpu.make_async_remote_copy(src_ref=src, dst_ref=dst, send_sem=ss, recv_sem=rs,
                                            device_id=where, device_id_type=MESH)

    def ks(q):
        return pl.ds(q * kc, kc)

    def far_row(d):
        return lax.rem(r + d, R)

    def near(dc):
        return lax.rem(c + dc + C, C)

    order = sorted(range(1, C), key=lambda d: -min(d, C - d))

    def slice_for(d, q):
        return pl.ds(far_row(d) * Kr + q * kc, kc)

    def own_a(q):
        return pltpu.make_async_copy(a_ref.at[slice_for(0, q)], a_all.at[0, ks(q)], arecv.at[0, q])

    def own_i(q):
        return pltpu.make_async_copy(i_ref.at[slice_for(0, q)], i_all.at[0, ks(q)], xrecv.at[0, q])

    for q in range(Q):
        own_a(q).start()
        own_i(q).start()

    barrier = pltpu.get_barrier_semaphore()
    partners = [{"row": far_row(d)} for d in range(1, R)]
    partners += [{"col": near(d)} for d in range(1, C)]
    partners += [{"layer": l ^ (1 << t)} for t in range(stages)]
    for p in partners:
        where = {"row": r, "col": c, "layer": l}
        where.update(p)
        pl.semaphore_signal(barrier, inc=1, device_id=where, device_id_type=MESH)
    pl.semaphore_wait(barrier, len(partners))

    def row_a(d, q):
        return remote(a_ref.at[slice_for(d, q)], a_all.at[R - d, ks(q)], asend.at[d, q], arecv.at[R - d, q], row=far_row(d))

    parts = [(0, early, (1 - top) * late)] + ([(early, late, top * early)] if late else [])

    def row_i(d, q, p):
        at, size, start = parts[p]
        src = i_ref.at[slice_for(d, q), :, pl.ds(pl.multiple_of(start, 128), size)] if late else i_ref.at[slice_for(d, q)]
        return remote(src, i_all.at[R - d, ks(q), :, pl.ds(at, size)], xsend.at[p * R + d, q], xrecv.at[p * R + R - d, q],
                      row=far_row(d))

    def col_a(d, j, q):
        b = far_row(d) * m + j
        at = pl.ds(j * V, V)
        src = a_all.at[d, ks(q), at] if d else a_ref.at[slice_for(0, q), at]
        return b, remote(src, az.at[c, ks(q)], zsend.at[d, j, q], zrecv.at[c, q], col=b)

    def col_start(d, q):
        for j in range(m):
            b, cp = col_a(d, j, q)

            @pl.when(b != c)
            def _():
                cp.start()

    for q in range(Q):
        for d in range(1, R):
            row_a(d, q).start()
        col_start(0, q)
    for p in range(len(parts)):
        for q in range(Q):
            for d in range(1, R):
                row_i(d, q, p).start()

    whole = (0, M, 0)

    def turn(d, q, part):
        first, size = part[:2]
        for k in range(kc):
            at = (q * kc + k) * V
            i_t[d, first:first + size, at:at + V] = i_all[d, q * kc + k, :, first:first + size].T

    def add(d, block, x, q, part):
        first, size, start = part
        piece = lax.dot_general(i_t[d, first:first + size, q * w:(q + 1) * w], x, (((1,), (0,)), ((), ())),
                                preferred_element_type=jnp.float32)
        to = pl.ds(start if isinstance(start, int) else pl.multiple_of(start, 128), size)
        if q == 0:
            acc[d, block, to] = piece
        else:
            acc[d, block, to] += piece

    own_row = lax.rem(lax.div(c, m) - r + R, R)
    own_at = pl.ds(pl.multiple_of(lax.rem(c, m) * V, V), V)

    def own_block(d, q, part):
        add(d, c, a_all[own_row, ks(q), own_at].reshape(w, N), q, part)

    for q in range(Q):
        own_a(q).wait()
        for d in range(1, R):
            row_a(R - d, q).wait_recv()
            col_start(d, q)
        own_i(q).wait()
        turn(0, q, whole)
        own_block(0, q, whole)

    for q in range(Q):
        for dc in order[::-1]:
            s = near(dc)
            here = az.at[s, ks(q)]
            remote(here, here, zsend.at[0, 0, q], zrecv.at[s, q], col=s).wait_recv()
            add(0, s, az[s, ks(q)].reshape(w, N), q, whole)

    def block(t, hi, bit):
        return (hi << (t + 1)) | (bit << t) | (l & ((1 << t) - 1))

    def halving(d, t, i, col):
        n = L >> (t + 1)
        hi = (l >> (t + 1)) ^ hi_order(n)[i]
        bit = (l >> t) & 1
        slot = n - 1 + hi
        give, keep = block(t, hi, 1 - bit), block(t, hi, bit)
        give, keep = (pl.ds(pl.multiple_of(b * rows, 8), rows) for b in (give, keep))
        if d == 0:
            cp = remote(acc.at[0, :, give], lay_buf.at[0, slot], osend.at[slot], orecv.at[slot], layer=l ^ (1 << t))
        else:
            cp = remote(acc.at[d, col, give], lay_buf.at[d, slot, col], lsend.at[d, slot, col], lrecv.at[d, slot, col],
                        layer=l ^ (1 << t))
        return cp, keep, slot

    def own_stage(t):
        for i in range(L >> (t + 1)):
            cp, keep, slot = halving(0, t, i, None)
            cp.wait_recv()
            acc[0, :, keep] += lay_buf[0, slot]
            if t + 1 < stages and i < L >> (t + 2):
                halving(0, t + 1, i, None)[0].start()

    for i in range(L >> 1):
        halving(0, 0, i, None)[0].start()

    c_order = [near(dc) for dc in order] + [c]
    mine = pl.ds(pl.multiple_of(l * rows, 8), rows)

    def first_stage_start(i):
        for d in range(1, R):
            for col in c_order:
                halving(d, 0, i, col)[0].start()

    def stage_end(t, i):
        for d in range(1, R):
            for col in c_order:
                cp, keep, slot = halving(d, t, i, col)
                cp.wait_recv()
                acc[d, col, keep] += lay_buf[d, slot, col]
                if t + 1 == stages:
                    row_sum(d, col).start()
                elif i < L >> (t + 2):
                    halving(d, t + 1, i, col)[0].start()

    for p, part in enumerate(parts):
        for q in range(Q):
            for d in range(1, R):
                row_i(R - d, q, p).wait_recv()
                turn(d, q, part)
                own_block(d, q, part)
                for dc in order:
                    s = near(dc)
                    add(d, s, az[s, ks(q)].reshape(w, N), q, part)
            if p == 0 and q == 0:
                own_stage(0)
            if p == 1 and q == min(1, Q - 1):
                stage_end(0, 0)
        if late:
            first_stage_start(p)

    def row_sum(d, col):
        return remote(acc.at[d, col, mine], row_buf.at[R - d, col], rsend.at[d, col], rrecv.at[R - d, col], row=far_row(d))

    def col_sum(dc):
        return remote(acc.at[0, near(dc), mine], col_buf.at[c], csend.at[dc], crecv.at[c], col=near(dc))

    if not late:
        for i in range(L >> 1):
            first_stage_start(i)
    for t in range(1, stages):
        own_stage(t)
    for t in range(stages):
        for i in range(L >> (t + 1)):
            if not (late and t == 0 and i == 0):
                stage_end(t, i)
    for at, col in enumerate(c_order):
        for d in range(1, R):
            row_sum(R - d, col).wait_recv()
            acc[0, col, mine] += row_buf[d, col]
        if at < C - 1:
            col_sum(order[at]).start()

    total = acc[0, c, mine]
    for dc in order[::-1]:
        s = near(dc)
        remote(col_buf.at[s], col_buf.at[s], csend.at[dc], crecv.at[s], col=s).wait_recv()
        total += col_buf[s]
    o_ref[...] = total

    for q in range(Q):
        for d in range(R):
            if d:
                row_a(d, q).wait_send()
                for p in range(len(parts)):
                    row_i(d, q, p).wait_send()
            for j in range(m):
                b, cp = col_a(d, j, q)

                @pl.when(b != c)
                def _():
                    cp.wait_send()
    for t in range(stages):
        for i in range(L >> (t + 1)):
            halving(0, t, i, None)[0].wait_send()
            for d in range(1, R):
                for col in c_order:
                    halving(d, t, i, col)[0].wait_send()
    for col in c_order:
        for d in range(1, R):
            row_sum(d, col).wait_send()
    for dc in order:
        col_sum(dc).wait_send()


def local(R, C, L, integrals, amplitudes, coulomb, row_gap, col_gap):
    K, V, M = integrals.shape
    V_row, N = amplitudes.shape[1:]
    rows = M // L
    Kr = K // R
    Q = Kr
    m = C // R
    slots = L - 1
    dma = pltpu.SemaphoreType.DMA
    vmem = pl.BlockSpec(memory_space=pltpu.VMEM)
    anyspace = pl.BlockSpec(memory_space=pl.ANY)
    own_rows = pl.pallas_call(
        functools.partial(kernel, R, C, L, Q),
        out_shape=jax.ShapeDtypeStruct((rows, N), jnp.float32),
        in_specs=[anyspace, anyspace],
        out_specs=vmem,
        scratch_shapes=[
            pltpu.VMEM((R, Kr, V_row, N), jnp.bfloat16),
            pltpu.VMEM((C, Kr, V, N), jnp.bfloat16),
            pltpu.VMEM((R, Kr, V, M), jnp.bfloat16),
            pltpu.VMEM((R, M, Kr * V), jnp.bfloat16),
            pltpu.VMEM((R, C, M, N), jnp.float32),
            pltpu.VMEM((R, slots, C, rows, N), jnp.float32),
            pltpu.VMEM((R, C, rows, N), jnp.float32),
            pltpu.VMEM((C, rows, N), jnp.float32),
            dma((R, Q)), dma((R, Q)),
            dma((2 * R, Q)), dma((2 * R, Q)),
            dma((R, m, Q)), dma((C, Q)),
            dma((slots,)), dma((slots,)),
            dma((R, slots, C)), dma((R, slots, C)),
            dma((R, C)), dma((R, C)),
            dma((C,)), dma((C,)),
        ],
        compiler_params=pltpu.CompilerParams(collective_id=0, has_side_effects=True),
    )(integrals, amplitudes)
    gap_sum = row_gap[:, None] + col_gap[None, :]
    return (coulomb.astype(jnp.float32) + own_rows) / gap_sum


def solution(mesh):
    R, C, L = (mesh.shape[a] for a in ("row", "col", "layer"))
    placed = (
        P("layer", "col", "row"),
        P("layer", "row", "col"),
        P(("row", "layer"), "col"),
        P(("row", "layer")),
        P("col"),
    )
    return jax.shard_map(
        functools.partial(local, R, C, L), mesh=mesh, in_specs=placed, out_specs=P(("row", "layer"), "col"),
        check_vma=False,
    )
```

```python
import functools

import jax
import jax.numpy as jnp
from jax import lax
from jax.experimental import pallas as pl
from jax.experimental.pallas import tpu as pltpu
from jax.sharding import PartitionSpec as P

MESH = pl.DeviceIdType.MESH


def hi_order(n):
    if n == 1:
        return [0]
    below = hi_order(n // 2)
    return [2 * x + 1 for x in below] + [2 * x for x in below]


def kernel(R, C, L, Q, i_ref, a_ref, o_ref,
           a_all, az, i_all, i_t, acc, lay_buf, row_buf, col_buf,
           asend, arecv, xsend, xrecv, zsend, zrecv,
           osend, orecv, lsend, lrecv, rsend, rrecv, csend, crecv):
    r, c, l = lax.axis_index("row"), lax.axis_index("col"), lax.axis_index("layer")
    K, V_row, N = a_ref.shape
    V, M = i_ref.shape[1:]
    Kr = K // R
    kc = Kr // Q
    m = C // R
    w = kc * V
    rows = M // L
    stages = L.bit_length() - 1
    late = M // 2 // 128 * 128 if stages == 2 and M % 128 == 0 else 0
    early = M - late
    top = l >> (stages - 1)

    def remote(src, dst, ss, rs, **to):
        where = {"row": r, "col": c, "layer": l}
        where.update(to)
        return pltpu.make_async_remote_copy(src_ref=src, dst_ref=dst, send_sem=ss, recv_sem=rs,
                                            device_id=where, device_id_type=MESH)

    def ks(q):
        return pl.ds(q * kc, kc)

    def far_row(d):
        return lax.rem(r + d, R)

    def near(dc):
        return lax.rem(c + dc + C, C)

    order = sorted(range(1, C), key=lambda d: -min(d, C - d))

    def slice_for(d, q):
        return pl.ds(far_row(d) * Kr + q * kc, kc)

    def own_a(q):
        return pltpu.make_async_copy(a_ref.at[slice_for(0, q)], a_all.at[0, ks(q)], arecv.at[0, q])

    def own_i(q):
        return pltpu.make_async_copy(i_ref.at[slice_for(0, q)], i_all.at[0, ks(q)], xrecv.at[0, q])

    for q in range(Q):
        own_a(q).start()
        own_i(q).start()

    barrier = pltpu.get_barrier_semaphore()
    partners = [{"row": far_row(d), "col": near(dc)} for d in range(R) for dc in range(C) if d or dc]
    partners += [{"layer": l ^ (1 << t)} for t in range(stages)]
    for p in partners:
        where = {"row": r, "col": c, "layer": l}
        where.update(p)
        pl.semaphore_signal(barrier, inc=1, device_id=where, device_id_type=MESH)
    pl.semaphore_wait(barrier, len(partners))

    def row_a(d, q):
        return remote(a_ref.at[slice_for(d, q)], a_all.at[R - d, ks(q)], asend.at[d, q], arecv.at[R - d, q], row=far_row(d))

    parts = [(0, early, (1 - top) * late)] + ([(early, late, top * early)] if late else [])

    def row_i(d, q, p):
        at, size, start = parts[p]
        src = i_ref.at[slice_for(d, q), :, pl.ds(pl.multiple_of(start, 128), size)] if late else i_ref.at[slice_for(d, q)]
        return remote(src, i_all.at[R - d, ks(q), :, pl.ds(at, size)], xsend.at[p * R + d, q], xrecv.at[p * R + R - d, q],
                      row=far_row(d))

    def col_a(d, j, q):
        b = far_row(d) * m + j
        at = pl.ds(j * V, V)
        src = a_all.at[d, ks(q), at] if d else a_ref.at[slice_for(0, q), at]
        return b, remote(src, az.at[c, ks(q)], zsend.at[d, j, q], zrecv.at[c, q], col=b)

    def col_start(d, q):
        for j in range(m):
            b, cp = col_a(d, j, q)

            @pl.when(b != c)
            def _():
                cp.start()

    for q in range(Q):
        for d in range(1, R):
            row_a(d, q).start()
        col_start(0, q)
    for p in range(len(parts)):
        for q in range(Q):
            for d in range(1, R):
                row_i(d, q, p).start()

    whole = (0, M, 0)

    def turn(d, q, part):
        first, size = part[:2]
        for k in range(kc):
            at = (q * kc + k) * V
            i_t[d, first:first + size, at:at + V] = i_all[d, q * kc + k, :, first:first + size].T

    def add(d, block, x, q, part):
        first, size, start = part
        piece = lax.dot_general(i_t[d, first:first + size, q * w:(q + 1) * w], x, (((1,), (0,)), ((), ())),
                                preferred_element_type=jnp.float32)
        to = pl.ds(start if isinstance(start, int) else pl.multiple_of(start, 128), size)
        if q == 0:
            acc[d, block, to] = piece
        else:
            acc[d, block, to] += piece

    own_row = lax.rem(lax.div(c, m) - r + R, R)
    own_at = pl.ds(pl.multiple_of(lax.rem(c, m) * V, V), V)

    def own_block(d, q, part):
        add(d, c, a_all[own_row, ks(q), own_at].reshape(w, N), q, part)

    for q in range(Q):
        own_a(q).wait()
        for d in range(1, R):
            row_a(R - d, q).wait_recv()
            col_start(d, q)
        own_i(q).wait()
        turn(0, q, whole)
        own_block(0, q, whole)

    for q in range(Q):
        for dc in order[::-1]:
            s = near(dc)
            here = az.at[s, ks(q)]
            remote(here, here, zsend.at[0, 0, q], zrecv.at[s, q], col=s).wait_recv()
            add(0, s, az[s, ks(q)].reshape(w, N), q, whole)

    def block(t, hi, bit):
        return (hi << (t + 1)) | (bit << t) | (l & ((1 << t) - 1))

    def halving(d, t, i, col):
        n = L >> (t + 1)
        hi = (l >> (t + 1)) ^ hi_order(n)[i]
        bit = (l >> t) & 1
        slot = n - 1 + hi
        give, keep = block(t, hi, 1 - bit), block(t, hi, bit)
        give, keep = (pl.ds(pl.multiple_of(b * rows, 8), rows) for b in (give, keep))
        if d == 0:
            cp = remote(acc.at[0, :, give], lay_buf.at[0, slot], osend.at[slot], orecv.at[slot], layer=l ^ (1 << t))
        else:
            cp = remote(acc.at[d, col, give], lay_buf.at[d, slot, col], lsend.at[d, slot, col], lrecv.at[d, slot, col],
                        layer=l ^ (1 << t))
        return cp, keep, slot

    def own_stage(t):
        for i in range(L >> (t + 1)):
            cp, keep, slot = halving(0, t, i, None)
            cp.wait_recv()
            acc[0, :, keep] += lay_buf[0, slot]
            if t + 1 < stages and i < L >> (t + 2):
                halving(0, t + 1, i, None)[0].start()

    for i in range(L >> 1):
        halving(0, 0, i, None)[0].start()

    c_order = [near(dc) for dc in order] + [c]
    mine = pl.ds(pl.multiple_of(l * rows, 8), rows)

    def first_stage_start(i):
        for d in range(1, R):
            for col in c_order:
                halving(d, 0, i, col)[0].start()

    def stage_end(t, i):
        for d in range(1, R):
            for col in c_order:
                cp, keep, slot = halving(d, t, i, col)
                cp.wait_recv()
                acc[d, col, keep] += lay_buf[d, slot, col]
                if t + 1 == stages:
                    row_sum(d, col).start()
                elif i < L >> (t + 2):
                    halving(d, t + 1, i, col)[0].start()

    for p, part in enumerate(parts):
        for q in range(Q):
            for d in range(1, R):
                row_i(R - d, q, p).wait_recv()
                turn(d, q, part)
                own_block(d, q, part)
                for dc in order:
                    s = near(dc)
                    add(d, s, az[s, ks(q)].reshape(w, N), q, part)
            if p == 0 and q == 0:
                own_stage(0)
            if p == 1 and q == min(1, Q - 1):
                stage_end(0, 0)
        if late:
            first_stage_start(p)

    def row_sum(d, col):
        return remote(acc.at[d, col, mine], row_buf.at[R - d, c], rsend.at[d, col], rrecv.at[R - d, c],
                      row=far_row(d), col=col)

    def col_sum(dc):
        return remote(acc.at[0, near(dc), mine], col_buf.at[c], csend.at[dc], crecv.at[c], col=near(dc))

    if not late:
        for i in range(L >> 1):
            first_stage_start(i)
    for t in range(1, stages):
        own_stage(t)
    for dc in order:
        col_sum(dc).start()
    for t in range(stages):
        for i in range(L >> (t + 1)):
            if not (late and t == 0 and i == 0):
                stage_end(t, i)
    total = acc[0, c, mine]
    for dc in order[::-1]:
        s = near(dc)
        remote(col_buf.at[s], col_buf.at[s], csend.at[dc], crecv.at[s], col=s).wait_recv()
        total += col_buf[s]
    for col in c_order[::-1]:
        for d in range(1, R):
            here = row_buf.at[d, col]
            remote(here, here, rsend.at[d, col], rrecv.at[d, col], row=far_row(d), col=col).wait_recv()
            total += row_buf[d, col]
    o_ref[...] = total

    for q in range(Q):
        for d in range(R):
            if d:
                row_a(d, q).wait_send()
                for p in range(len(parts)):
                    row_i(d, q, p).wait_send()
            for j in range(m):
                b, cp = col_a(d, j, q)

                @pl.when(b != c)
                def _():
                    cp.wait_send()
    for t in range(stages):
        for i in range(L >> (t + 1)):
            halving(0, t, i, None)[0].wait_send()
            for d in range(1, R):
                for col in c_order:
                    halving(d, t, i, col)[0].wait_send()
    for col in c_order:
        for d in range(1, R):
            row_sum(d, col).wait_send()
    for dc in order:
        col_sum(dc).wait_send()


def local(R, C, L, integrals, amplitudes, coulomb, row_gap, col_gap):
    K, V, M = integrals.shape
    V_row, N = amplitudes.shape[1:]
    rows = M // L
    Kr = K // R
    Q = Kr
    m = C // R
    slots = L - 1
    dma = pltpu.SemaphoreType.DMA
    vmem = pl.BlockSpec(memory_space=pltpu.VMEM)
    anyspace = pl.BlockSpec(memory_space=pl.ANY)
    own_rows = pl.pallas_call(
        functools.partial(kernel, R, C, L, Q),
        out_shape=jax.ShapeDtypeStruct((rows, N), jnp.float32),
        in_specs=[anyspace, anyspace],
        out_specs=vmem,
        scratch_shapes=[
            pltpu.VMEM((R, Kr, V_row, N), jnp.bfloat16),
            pltpu.VMEM((C, Kr, V, N), jnp.bfloat16),
            pltpu.VMEM((R, Kr, V, M), jnp.bfloat16),
            pltpu.VMEM((R, M, Kr * V), jnp.bfloat16),
            pltpu.VMEM((R, C, M, N), jnp.float32),
            pltpu.VMEM((R, slots, C, rows, N), jnp.float32),
            pltpu.VMEM((R, C, rows, N), jnp.float32),
            pltpu.VMEM((C, rows, N), jnp.float32),
            dma((R, Q)), dma((R, Q)),
            dma((2 * R, Q)), dma((2 * R, Q)),
            dma((R, m, Q)), dma((C, Q)),
            dma((slots,)), dma((slots,)),
            dma((R, slots, C)), dma((R, slots, C)),
            dma((R, C)), dma((R, C)),
            dma((C,)), dma((C,)),
        ],
        compiler_params=pltpu.CompilerParams(collective_id=0, has_side_effects=True),
    )(integrals, amplitudes)
    gap_sum = row_gap[:, None] + col_gap[None, :]
    return (coulomb.astype(jnp.float32) + own_rows) / gap_sum


def solution(mesh):
    R, C, L = (mesh.shape[a] for a in ("row", "col", "layer"))
    placed = (
        P("layer", "col", "row"),
        P("layer", "row", "col"),
        P(("row", "layer"), "col"),
        P(("row", "layer")),
        P("col"),
    )
    return jax.shard_map(
        functools.partial(local, R, C, L), mesh=mesh, in_specs=placed, out_specs=P(("row", "layer"), "col"),
        check_vma=False,
    )
```
